256 devices in a mesh: sec: 8 (over z_lo, core), ctx: 32 (over z_hi, x, y).
Axes of the slice: x: 4, y: 4, z: 8 (z_hi: 2, z_lo: 4; z = z_hi * 4 + z_lo), core: 2. Of those that a mesh axis runs over, the one named last changes fastest.
Arguments:
- q_frames: bfloat16 [8, 512, 8, 3584], P('sec', 'ctx'), may hold values from -8 to 8
- k_frames: bfloat16 [8, 512, 8, 512], P('sec', 'ctx'), may hold values from -8 to 8
- v_frames: bfloat16 [8, 512, 8, 512], P('sec', 'ctx'), may hold values from -6 to 6
- video_frames: int32 [8], replicated, may hold values from 256 to 512, as said below
- frame_section: int32 [8, 512], P('sec', 'ctx'), may hold values from 0 to 7, as said below
- frame_offset: int32 [8, 512], P('sec', 'ctx'), may hold values from 0 to 4088, as said below
Outputs:
- attention_out: bfloat16 [8, 4096, 3584], P('sec', 'ctx')
The draws below stay inside these ranges and needn't reach their ends.
Inputs may be any that keep to these rules, and one draw needn't show every extreme that they name: `video_frames`: at least one section's video fills all 512 slots. `frame_section`: every device holds exactly 2 frame slots for each section. `frame_offset`: A multiple of 8; it falls in the 128 positions of the section's device whose ctx index equals that of the slot's device; the slots of one section cover its positions once. Slots at positions of frames beyond the video's length are not part of it.
All inputs are finite; a program needn't handle non-finite values.
Results may differ from the reference program's by a relative error of at most 0.006.
Values may be sent and summed in bfloat16 or wider, within the bound.
No kernel may reach another device: no remote copies, remote signals or barrier semaphores. Data moves between devices by JAX's collectives and lax.ppermute only.
A program may use at most 128 MiB of HBM per device.

```python
import math
import jax
import jax.numpy as jnp
from jax import lax

HEADS = 28
KV_HEADS = 4
HEAD_DIM = 128
TPF = 8
FPD = 16
GROUP = 7
CAP = 2
CYCLE_FRAMES = 512
SEQ = 4096
N_SEC = 8
N_CTX = 32


def routing_tables(key):
    base = jax.random.fold_in(key, 11)
    shift_key, order_key = jax.random.split(base)
    shifts = jax.vmap(lambda subkey: jax.random.permutation(subkey, N_SEC))(jax.random.split(shift_key, N_CTX))
    orders = jax.vmap(lambda subkey: jax.random.permutation(subkey, FPD))(jax.random.split(order_key, N_SEC * N_CTX))
    orders = orders.reshape(N_SEC, N_CTX, FPD)
    source_sec = jnp.arange(N_SEC, dtype=jnp.int32)[:, None, None]
    place = jnp.arange(N_CTX, dtype=jnp.int32)[None, :, None]
    slot_ids = jnp.arange(FPD, dtype=jnp.int32)[None, None, :]
    group_ids = slot_ids // CAP
    section = (source_sec + shifts[place, group_ids]) % N_SEC
    within = orders[section, place, slot_ids]
    offset = (place * FPD + within) * TPF
    return (section.reshape(N_SEC, CYCLE_FRAMES).astype(jnp.int32), offset.reshape(N_SEC, CYCLE_FRAMES).astype(jnp.int32))


def draw_frame_section(key, part):
    return routing_tables(key)[0]


def draw_frame_offset(key, part):
    return routing_tables(key)[1]


def draw_video_frames(key, part):
    base = jax.random.fold_in(key, 23)
    count_key, pick_key = jax.random.split(base)
    counts = jax.random.randint(count_key, (N_SEC,), CYCLE_FRAMES // 2, CYCLE_FRAMES + 1)
    fullest = jax.random.randint(pick_key, (), 0, N_SEC)
    return jnp.where(jnp.arange(N_SEC) == fullest, CYCLE_FRAMES, counts).astype(jnp.int32)


def query_key(key):
    base = jax.random.fold_in(key, 37)
    parts = jax.random.split(base, 2)
    q_shape = (N_SEC, CYCLE_FRAMES, TPF, HEADS * HEAD_DIM)
    k_shape = (N_SEC, CYCLE_FRAMES, TPF, KV_HEADS * HEAD_DIM)
    queries = jnp.clip(jax.random.normal(parts[0], q_shape, jnp.float32), -6.0, 6.0)
    keys = jnp.clip(jax.random.normal(parts[1], k_shape, jnp.float32), -6.0, 6.0)
    return (queries, keys)


def draw_q_frames(key, part):
    return query_key(key)[0].astype(jnp.bfloat16)


def draw_k_frames(key, part):
    return query_key(key)[1].astype(jnp.bfloat16)


def level_of(own_key, extent, shards, least, top_value):
    factor_of, own = 1.0, jax.random.fold_in(own_key, 6)
    for axis_at, blocks in shards:
        heights = jnp.exp(jax.random.uniform(jax.random.fold_in(own, axis_at), (blocks,), jnp.float32, least / len(shards), top_value / len(shards)))
        factor_of = factor_of * jnp.repeat(heights, extent[axis_at] // blocks).reshape([-1 if axis == axis_at else 1 for axis in range(len(extent))])
    return factor_of


def bell_draw(stream_key, dims, deviation, bound, cuts=(), kind=jnp.bfloat16):
    values = jax.random.normal(stream_key, dims, jnp.float32) * deviation
    if len(cuts) > 0:
        values = level_of(stream_key, dims, cuts, -0.22, 0.18) * values
    return jnp.clip(values, min=-bound, max=bound).astype(kind)


def setup_inputs(seed: int = 0) -> dict:
    splits = jax.random.split(jax.random.key(seed), 7)
    return {
        "q_frames": draw_q_frames(jax.random.fold_in(splits[6], 71), 0),
        "k_frames": draw_k_frames(jax.random.fold_in(splits[6], 71), 0),
        "v_frames": bell_draw(splits[2], (N_SEC, CYCLE_FRAMES, TPF, KV_HEADS * HEAD_DIM), 1.0, 6.0, ((0, 8), (1, 32))),
        "video_frames": draw_video_frames(jax.random.fold_in(splits[6], 71), 0),
        "frame_section": draw_frame_section(jax.random.fold_in(splits[6], 71), 0),
        "frame_offset": draw_frame_offset(jax.random.fold_in(splits[6], 71), 0),
    }


floor_score = -1e+30

def reference(q_frames, k_frames, v_frames, video_frames, frame_section, frame_offset):
    section_of = frame_section.astype(jnp.int32)
    slot_of = (frame_offset // TPF).astype(jnp.int32)
    width_q = q_frames.shape[-1]
    width_k = k_frames.shape[-1]
    q_seq = jnp.zeros((N_SEC, CYCLE_FRAMES, TPF, width_q), q_frames.dtype).at[section_of, slot_of].set(q_frames).reshape(N_SEC, SEQ, width_q)
    k_seq = jnp.zeros((N_SEC, CYCLE_FRAMES, TPF, width_k), k_frames.dtype).at[section_of, slot_of].set(k_frames).reshape(N_SEC, SEQ, width_k)
    v_seq = jnp.zeros((N_SEC, CYCLE_FRAMES, TPF, width_k), v_frames.dtype).at[section_of, slot_of].set(v_frames).reshape(N_SEC, SEQ, width_k)
    score_scale = 1.0 / math.sqrt(HEAD_DIM)
    block = math.gcd(SEQ, 512)
    positions = jnp.arange(SEQ, dtype=jnp.int32)

    def one_section(inputs):
        q_all, k_all, v_all, frames = inputs
        live_len = frames * TPF
        key_rows = k_all.astype(jnp.float32).reshape(SEQ, KV_HEADS, HEAD_DIM)
        value_rows = v_all.astype(jnp.float32).reshape(SEQ, KV_HEADS, HEAD_DIM)

        def one_block(block_start):
            queries = lax.dynamic_slice_in_dim(q_all, block_start, block, 0).astype(jnp.float32)
            queries = queries.reshape(block, KV_HEADS, GROUP, HEAD_DIM)
            query_pos = block_start + jnp.arange(block, dtype=jnp.int32)
            scores = jnp.einsum('rkgd,nkd->kgrn', queries, key_rows, precision=lax.Precision.HIGHEST) * score_scale
            visible = (positions[None, :] <= query_pos[:, None]) & (positions[None, :] < live_len)
            masked = jnp.where(visible, scores, floor_score)
            row_max = lax.optimization_barrier(jnp.max(masked, axis=-1, keepdims=True))
            weights = jnp.where(visible, jnp.exp(scores - row_max), 0.0)
            weight_sum = lax.optimization_barrier(jnp.sum(weights, axis=-1))
            rounded = lax.optimization_barrier(weights.astype(jnp.bfloat16)).astype(jnp.float32)
            mixed = jnp.einsum('kgrn,nkd->rkgd', rounded, value_rows, precision=lax.Precision.HIGHEST)
            mixed = mixed / jnp.transpose(weight_sum, (2, 0, 1))[..., None]
            mixed = mixed.reshape(block, KV_HEADS * GROUP * HEAD_DIM)
            return jnp.where((query_pos < live_len)[:, None], mixed, 0.0).astype(jnp.bfloat16)
        starts = jnp.arange(0, SEQ, block, dtype=jnp.int32)
        return lax.map(one_block, starts).reshape(SEQ, width_q)
    return lax.map(one_section, (q_seq, k_seq, v_seq, video_frames.astype(jnp.int32)))
```

```python
import functools
import math

import jax
import jax.numpy as jnp
from jax import lax
from jax.experimental import pallas as pl
from jax.experimental.pallas import tpu as pltpu
from jax.sharding import Mesh, PartitionSpec as P

SEC = ("zl", "core")
BLOCK = 128
LANES = 128
GROUP = 7
HEADS_KV = 4
NEG = -1e30
VMEM_LIMIT = 56 * 1024 * 1024


def slot_order(sec_ref, order_ref, count_ref):
    for s in range(8):
        count_ref[s] = 0

    def body(i, _):
        s = sec_ref[0, i]
        c = count_ref[s]
        order_ref[2 * s + c] = i
        count_ref[s] = c + 1
        return 0

    lax.fori_loop(0, 16, body, 0)


def prep_kv_kernel(sec_ref, k_ref, v_ref, out_ref, order_ref, count_ref):
    slot_order(sec_ref, order_ref, count_ref)
    for s in range(8):
        a, b = order_ref[2 * s], order_ref[2 * s + 1]
        for row, ref in ((0, k_ref), (16, v_ref)):
            both = jnp.concatenate([ref[0, a], ref[0, b]], axis=0)
            for h in range(HEADS_KV):
                piece = both[:, h * LANES : (h + 1) * LANES]
                for zh in range(2):
                    out_ref[(zh * 4 + h) * 8 + s, row : row + 16, :] = piece


def prep_q_kernel(sec_ref, off_ref, q_ref, out_ref, order_ref, count_ref):
    slot_order(sec_ref, order_ref, count_ref)
    me = lax.axis_index("zl") * 2 + lax.axis_index("core")
    rel = lax.broadcasted_iota(jnp.int32, (8, LANES), 1) - 16 * me
    for s in range(8):
        a, b = order_ref[2 * s], order_ref[2 * s + 1]
        pos_a = jnp.bitwise_and(off_ref[0, a], BLOCK - 1)
        pos_b = jnp.bitwise_and(off_ref[0, b], BLOCK - 1)
        pos = jnp.where(rel < 8, pos_a + rel, pos_b + rel - 8)
        pos = jnp.where((rel >= 0) & (rel < 16), pos, 0)
        pos = pos.astype(jnp.float32).astype(jnp.bfloat16)
        both = jnp.concatenate([q_ref[0, a], q_ref[0, b]], axis=0)
        for h in range(HEADS_KV):
            for g in range(GROUP):
                col = (h * GROUP + g) * LANES
                out_ref[h * 8 + s, g * 16 : (g + 1) * 16, :] = both[:, col : col + LANES]
            out_ref[h * 8 + s, GROUP * 16 :, :] = pos


def attend_kernel(
    shifts,
    video_ref,
    q_ref,
    own_ref,
    prev_ref,
    next_ref,
    far0_ref,
    far1_ref,
    out_ref,
    kv_s,
    q_s,
    s_s,
    max_s,
    sum_s,
    acc_s,
    sem,
):
    x, y, zh = lax.axis_index("x"), lax.axis_index("y"), lax.axis_index("zh")
    me = lax.axis_index("zl") * 2 + lax.axis_index("core")
    live = video_ref[me] * 8
    rows = GROUP * BLOCK
    factor = math.log2(math.e) / math.sqrt(128.0)

    copies = []
    for a, ref in enumerate((own_ref, prev_ref, next_ref)):
        for zp in range(2):
            copies.append((ref.at[pl.ds(zp * 32, 32)], (zp * 4 + a) * 32))
    copies.append((far0_ref, 3 * 32))
    copies.append((far1_ref, 7 * 32))
    started = []
    for i, (src, at) in enumerate(copies):
        copy = pltpu.make_async_copy(src, kv_s.at[pl.ds(at, 32)], sem.at[i])
        copy.start()
        started.append(copy)
    for copy in started:
        copy.wait()

    row_pos = lax.broadcasted_iota(jnp.int32, (BLOCK, LANES), 0).astype(jnp.float32)

    def one_block(i, xb):
        block = zh * 16 + xb * 4 + y
        block_live = block * BLOCK < live

        @pl.when(jnp.logical_not(block_live))
        def _():
            out_ref[i] = jnp.zeros((BLOCK, rows), jnp.bfloat16)

        @pl.when(block_live)
        def _():
            meta = q_ref[pl.ds(xb * 8, 8), GROUP * 16 :, :].astype(jnp.float32)
            pos = jnp.sum(meta, axis=0)[0:1]
            pick = (row_pos == pos).astype(jnp.float32).astype(jnp.bfloat16)
            for g in range(GROUP):
                raw = q_ref[pl.ds(xb * 8, 8), g * 16 : (g + 1) * 16, :].reshape(BLOCK, LANES)
                q_s[g * BLOCK : (g + 1) * BLOCK, :] = jnp.dot(
                    pick, raw, preferred_element_type=jnp.float32
                ).astype(jnp.bfloat16)
            max_s[...] = jnp.full((rows, LANES), NEG, jnp.float32)
            sum_s[...] = jnp.zeros((rows, LANES), jnp.float32)
            acc_s[...] = jnp.zeros((rows, LANES), jnp.float32)
            alive = block * BLOCK + pos.astype(jnp.int32) < live
            diag_pos = jnp.where(alive, pos, 1e9)

            def scores(j, width, bounds):
                keys = kv_s[pl.ds(j * 32, width // 16), 0:16, :].reshape(width, LANES)
                s = lax.dot_general(
                    q_s[...], keys, (((1,), (1,)), ((), ())), preferred_element_type=jnp.float32
                )
                top = None
                for c in range(width // LANES):
                    part = s[:, c * LANES : (c + 1) * LANES]
                    if bounds is not None:
                        seen = (bounds[c] <= row_pos)[None]
                        part = jnp.where(
                            seen, part.reshape(GROUP, BLOCK, LANES), NEG
                        ).reshape(rows, LANES)
                    s_s[j, :, c * LANES : (c + 1) * LANES] = part
                    top = part if top is None else jnp.maximum(top, part)
                max_s[...] = jnp.maximum(max_s[...], top)

            def mix(j, width):
                values = kv_s[pl.ds(j * 32, width // 16), 16:32, :].reshape(width, LANES)
                top = max_s[...]
                parts, total = [], None
                for c in range(width // LANES):
                    p = jnp.exp2(s_s[j, :, c * LANES : (c + 1) * LANES] * factor - top)
                    total = p if total is None else total + p
                    parts.append(p.astype(jnp.bfloat16))
                sum_s[...] += total
                acc_s[...] += jnp.dot(
                    jnp.concatenate(parts, axis=1), values, preferred_element_type=jnp.float32
                )

            def each(full, part):
                @pl.when(zh == 1)
                def _():
                    lax.fori_loop(0, 4, lambda j, _: (full(j), 0)[1], 0)

                def own(a, _):
                    ya = jnp.bitwise_and(y + jnp.where(a == 0, 0, jnp.where(a == 1, 3, a - 1)), 3)
                    n = xb + (ya <= y).astype(jnp.int32)
                    part(zh * 4 + a, ya, n)
                    return 0

                lax.fori_loop(0, 4, own, 0)

            def part_scores(j, ya, n):
                bounds = []
                for xp in range(4):
                    all_seen = (xp < xb) | ((xp == xb) & (ya < y))
                    diag = (xp == xb) & (ya == y)
                    bound = jnp.where(diag, diag_pos, jnp.where(all_seen, -1.0, 1e9))
                    bounds.append(bound)

                @pl.when(n > 2)
                def _():
                    scores(j, 512, bounds)

                @pl.when((n > 0) & (n <= 2))
                def _():
                    scores(j, 256, bounds)

            def part_mix(j, ya, n):
                @pl.when(n > 2)
                def _():
                    mix(j, 512)

                @pl.when((n > 0) & (n <= 2))
                def _():
                    mix(j, 256)

            each(lambda j: scores(j, 512, None), part_scores)
            top = jnp.max(max_s[...], axis=1, keepdims=True) * factor
            max_s[...] = jnp.broadcast_to(top, (rows, LANES))
            each(lambda j: mix(j, 512), part_mix)
            total = jnp.sum(sum_s[...], axis=1, keepdims=True)
            out = acc_s[...] / total
            row_live = row_pos < (live - block * BLOCK).astype(jnp.float32)
            for g in range(GROUP):
                piece = jnp.where(row_live, out[g * BLOCK : (g + 1) * BLOCK], 0.0)
                out_ref[i, :, g * LANES : (g + 1) * LANES] = piece.astype(jnp.bfloat16)

    for i, shift in enumerate(shifts):
        one_block(i, jnp.bitwise_and(x + shift, 3))


def join_kernel(a_ref, b_ref, c_ref, d_ref, out_ref, sem):
    x = lax.axis_index("x")
    copies = []
    for k, ref in enumerate((a_ref, b_ref, c_ref, d_ref)):
        head = jnp.bitwise_and(x + 4 - k, 3)
        col = pl.multiple_of(head * (GROUP * LANES), LANES)
        copy = pltpu.make_async_copy(
            ref.at[0], out_ref.at[0, :, pl.ds(col, GROUP * LANES)], sem.at[k]
        )
        copy.start()
        copies.append(copy)
    for copy in copies:
        copy.wait()


def vmem():
    return pl.BlockSpec(memory_space=pltpu.VMEM)


def smem():
    return pl.BlockSpec(memory_space=pltpu.SMEM)


def anywhere():
    return pl.BlockSpec(memory_space=pl.ANY)


def params():
    return pltpu.CompilerParams(vmem_limit_bytes=VMEM_LIMIT)


def exchange(value, axes):
    return lax.all_to_all(value, axes, split_axis=0, concat_axis=0, tiled=True)


def shift(value, axis, by):
    return lax.ppermute(value, axis, [(i, (i + by) % 4) for i in range(4)])


def local(q_frames, k_frames, v_frames, video_frames, frame_section, frame_offset):
    order = [pltpu.SMEM((16,), jnp.int32), pltpu.SMEM((8,), jnp.int32)]
    kv_send = pl.pallas_call(
        prep_kv_kernel,
        out_shape=jax.ShapeDtypeStruct((64, 32, LANES), jnp.bfloat16),
        in_specs=[smem(), vmem(), vmem()],
        out_specs=vmem(),
        scratch_shapes=order,
        compiler_params=params(),
        name="prep_kv",
    )(frame_section, k_frames, v_frames)
    q_send = pl.pallas_call(
        prep_q_kernel,
        out_shape=jax.ShapeDtypeStruct((32, GROUP * 16 + 8, LANES), jnp.bfloat16),
        in_specs=[smem(), smem(), vmem()],
        out_specs=vmem(),
        scratch_shapes=order,
        compiler_params=params(),
        name="prep_q",
    )(frame_section, frame_offset, q_frames)
    own = exchange(kv_send, ("zh", "x", "zl", "core"))
    q_send, own = lax.optimization_barrier((q_send, own))
    q_got = exchange(q_send, ("x", "zl", "core"))
    prev, nxt = shift(own, "y", 1), shift(own, "y", -1)
    far0, far1 = shift(prev[:32], "y", 1), shift(nxt[32:], "y", -1)

    def attend(shifts):
        rows = GROUP * BLOCK
        return pl.pallas_call(
            functools.partial(attend_kernel, shifts),
            out_shape=jax.ShapeDtypeStruct((len(shifts), BLOCK, rows), jnp.bfloat16),
            in_specs=[smem(), vmem()] + [anywhere()] * 5,
            out_specs=vmem(),
            scratch_shapes=[
                pltpu.VMEM((256, 32, LANES), jnp.bfloat16),
                pltpu.VMEM((rows, LANES), jnp.bfloat16),
                pltpu.VMEM((8, rows, 512), jnp.float32),
                pltpu.VMEM((rows, LANES), jnp.float32),
                pltpu.VMEM((rows, LANES), jnp.float32),
                pltpu.VMEM((rows, LANES), jnp.float32),
                pltpu.SemaphoreType.DMA((8,)),
            ],
            compiler_params=params(),
            cost_estimate=pl.CostEstimate(
                flops=2 * 2 * rows * 4096 * LANES,
                transcendentals=rows * 4096,
                bytes_accessed=3 << 20,
            ),
            name="attend",
        )(video_frames, q_got, own, prev, nxt, far0, far1)

    parts = {}
    for k in (1, 2, 3, 0):
        part = attend((k,))
        parts[k] = shift(part, "x", k) if k else part
    return pl.pallas_call(
        join_kernel,
        out_shape=jax.ShapeDtypeStruct((1, BLOCK, HEADS_KV * GROUP * LANES), jnp.bfloat16),
        in_specs=[anywhere()] * 4,
        out_specs=anywhere(),
        scratch_shapes=[pltpu.SemaphoreType.DMA((4,))],
        compiler_params=params(),
        name="join",
    )(parts[0], parts[1], parts[2], parts[3])


def solution(mesh):
    fine = Mesh(mesh.devices.reshape(4, 2, 2, 4, 4), ("zl", "core", "zh", "x", "y"))
    ctx = ("zh", "x", "y")
    return jax.shard_map(
        local,
        mesh=fine,
        in_specs=(
            P(SEC, ctx, None, None),
            P(SEC, ctx, None, None),
            P(SEC, ctx, None, None),
            P(),
            P(SEC, ctx),
            P(SEC, ctx),
        ),
        out_specs=P(SEC, ctx, None),
        check_vma=False,
    )
```

```python
import functools
import math

import jax
import jax.numpy as jnp
from jax import lax
from jax.experimental import pallas as pl
from jax.experimental.pallas import tpu as pltpu
from jax.sharding import Mesh, PartitionSpec as P

SEC = ("zl", "core")
BLOCK = 128
LANES = 128
GROUP = 7
HEADS_KV = 4
NEG = -1e30
VMEM_LIMIT = 24 * 1024 * 1024
VMEM_ALL = 56 * 1024 * 1024
TILE = 512


def slot_order(sec_ref, order_ref, count_ref):
    for s in range(8):
        count_ref[s] = 0

    def body(i, _):
        s = sec_ref[0, i]
        c = count_ref[s]
        order_ref[2 * s + c] = i
        count_ref[s] = c + 1
        return 0

    lax.fori_loop(0, 16, body, 0)


def prep_kv_kernel(sec_ref, k_ref, v_ref, out_ref, order_ref, count_ref):
    slot_order(sec_ref, order_ref, count_ref)
    for s in range(8):
        a, b = order_ref[2 * s], order_ref[2 * s + 1]
        for row, ref in ((0, k_ref), (16, v_ref)):
            both = jnp.concatenate([ref[0, a], ref[0, b]], axis=0)
            for h in range(HEADS_KV):
                for zh in range(2):
                    out_ref[(zh * 4 + h) * 8 + s, row : row + 16, :] = both[:, h * LANES : (h + 1) * LANES]


def prep_q_kernel(sec_ref, off_ref, q_ref, out_ref, order_ref, count_ref):
    slot_order(sec_ref, order_ref, count_ref)
    me = lax.axis_index("zl") * 2 + lax.axis_index("core")
    rel = lax.broadcasted_iota(jnp.int32, (8, LANES), 1) - 16 * me
    for s in range(8):
        a, b = order_ref[2 * s], order_ref[2 * s + 1]
        pos_a = jnp.bitwise_and(off_ref[0, a], BLOCK - 1)
        pos_b = jnp.bitwise_and(off_ref[0, b], BLOCK - 1)
        pos = jnp.where(rel < 8, pos_a + rel, pos_b + rel - 8)
        pos = jnp.where((rel >= 0) & (rel < 16), pos, 0)
        pos = pos.astype(jnp.float32).astype(jnp.bfloat16)
        both = jnp.concatenate([q_ref[0, a], q_ref[0, b]], axis=0)
        for h in range(HEADS_KV):
            for g in range(GROUP):
                col = (h * GROUP + g) * LANES
                out_ref[h * 8 + s, g * 16 : (g + 1) * 16, :] = both[:, col : col + LANES]
            out_ref[h * 8 + s, GROUP * 16 :, :] = pos


def arrange_kernel(*refs):
    sources, kv_ref = refs[:5], refs[5]
    copies = []
    for p in range(2):
        own, prev, nxt, far_k, far_v = sources
        for xp in range(4):
            at = pl.ds((p * 4 + xp) * 8, 8)
            for a, src in enumerate((own, prev, nxt)):
                copies.append((src.at[at], kv_ref.at[p * 4 + xp, a]))
            copies.append((far_k.at[at], kv_ref.at[p * 4 + xp, 3, :, 0:16]))
            copies.append((far_v.at[at], kv_ref.at[p * 4 + xp, 3, :, 16:32]))
    for src, dst in copies:
        dst[...] = src[...]


def attend_kernel(
    shifts, video_ref, q_ref, kv_ref, *refs
):
    out_refs = refs[: len(shifts)]
    q_s, mask_s, s0, s1, top0, top1, max_s, sum_s, acc_s = refs[len(shifts) :]
    x, y, zh = lax.axis_index("x"), lax.axis_index("y"), lax.axis_index("zh")
    me = lax.axis_index("zl") * 2 + lax.axis_index("core")
    live = video_ref[me] * 8
    rows = GROUP * BLOCK
    factor = math.log2(math.e) / math.sqrt(128.0)
    down = lax.broadcasted_iota(jnp.int32, (BLOCK, LANES), 0)
    across = lax.broadcasted_iota(jnp.int32, (BLOCK, LANES), 1)

    def dot(a, b, ca, cb):
        return lax.dot_general(
            a, b, (((ca,), (cb,)), ((), ())), preferred_element_type=jnp.float32
        )

    def scores(t, s_ref, top_ref):
        s = dot(kv_ref[t, :, :, 0:16, :].reshape(TILE, LANES), q_s[...], 1, 0)
        s_ref[...] = s
        top_ref[...] = jnp.max(s.reshape(TILE // 8, 8, rows), axis=0)

    def absorb(t, s, top):
        old = max_s[...]
        new = jnp.maximum(old, jnp.max(top, axis=0, keepdims=True) * factor)
        keep = jnp.exp2(old - new)
        max_s[...] = new
        p = jnp.exp2(s * factor - new)
        sum_s[...] = sum_s[...] * keep + jnp.sum(p, axis=0, keepdims=True)
        mixed = dot(kv_ref[t, :, :, 16:32, :].reshape(TILE, LANES), p.astype(jnp.bfloat16), 0, 0)
        acc_s[...] = acc_s[...] * keep + mixed

    def absorb_last(t, s_ref):
        s = s_ref[...] + jnp.concatenate([mask_s[...]] * GROUP, axis=1)
        absorb(t, s, jnp.max(s.reshape(TILE // 8, 8, rows), axis=0))

    def one_block(out_ref, xb):
        block = zh * 16 + xb * 4 + y
        block_live = block * BLOCK < live

        @pl.when(jnp.logical_not(block_live))
        def _():
            out_ref[0] = jnp.zeros((BLOCK, rows), jnp.bfloat16)

        @pl.when(block_live)
        def _():
            first = 0
            last = zh * 4 + xb
            meta = q_ref[pl.ds(xb * 8, 8), GROUP * 16 :, :].astype(jnp.float32)
            pos = jnp.sum(meta, axis=0)[0:1]
            pick = (down.astype(jnp.float32) == pos).astype(jnp.float32).astype(jnp.bfloat16)
            for g in range(GROUP):
                raw = q_ref[pl.ds(xb * 8, 8), g * 16 : (g + 1) * 16, :].reshape(BLOCK, LANES)
                q_s[:, g * BLOCK : (g + 1) * BLOCK] = dot(raw, pick, 0, 1).astype(jnp.bfloat16)
            reach = (down <= across) & (block * BLOCK + down < live)
            seen = dot(pick, reach.astype(jnp.float32).astype(jnp.bfloat16), 0, 0)
            mask_s[0:BLOCK, :] = jnp.where(seen > 0.5, 0.0, NEG)
            for a, by in ((1, 3), (2, 1), (3, 2)):
                before = jnp.bitwise_and(y + by, 3) < y
                mask_s[a * BLOCK : (a + 1) * BLOCK, :] = jnp.full(
                    (BLOCK, LANES), jnp.where(before, 0.0, NEG)
                )
            max_s[...] = jnp.full((1, rows), NEG, jnp.float32)
            sum_s[...] = jnp.zeros((1, rows), jnp.float32)
            acc_s[...] = jnp.zeros((LANES, rows), jnp.float32)

            scores(first, s0, top0)
            full = last - first

            def pair(n, _):
                t = first + 2 * n
                scores(t + 1, s1, top1)
                absorb(t, s0[...], top0[...])
                scores(t + 2, s0, top0)
                absorb(t + 1, s1[...], top1[...])
                return 0

            lax.fori_loop(0, lax.shift_right_logical(full, 1), pair, 0)
            odd = jnp.bitwise_and(full, 1) == 1

            @pl.when(odd)
            def _():
                scores(last, s1, top1)
                absorb(last - 1, s0[...], top0[...])
                absorb_last(last, s1)

            @pl.when(jnp.logical_not(odd))
            def _():
                absorb_last(last, s0)

            out = acc_s[...] / sum_s[...]
            row_live = block * BLOCK + down < live
            for g in range(GROUP):
                piece = jnp.where(row_live, out[:, g * BLOCK : (g + 1) * BLOCK].T, 0.0)
                out_ref[0, :, g * LANES : (g + 1) * LANES] = piece.astype(jnp.bfloat16)

    for out_ref, k in zip(out_refs, shifts):
        one_block(out_ref, jnp.bitwise_xor(x, k))


def join_kernel(a_ref, b_ref, c_ref, d_ref, out_ref):
    x = lax.axis_index("x")
    for k, ref in enumerate((a_ref, b_ref, c_ref, d_ref)):
        head = jnp.bitwise_xor(x, k)
        col = pl.multiple_of(head * (GROUP * LANES), LANES)
        out_ref[0, :, pl.ds(col, GROUP * LANES)] = ref[0]


def vmem():
    return pl.BlockSpec(memory_space=pltpu.VMEM)


def smem():
    return pl.BlockSpec(memory_space=pltpu.SMEM)


def anywhere():
    return pl.BlockSpec(memory_space=pl.ANY)


def params(limit=VMEM_LIMIT):
    return pltpu.CompilerParams(vmem_limit_bytes=limit)


def exchange(value, axes):
    return lax.all_to_all(value, axes, split_axis=0, concat_axis=0, tiled=True)


def shift(value, axis, by):
    return lax.ppermute(value, axis, [(i, (i + by) % 4) for i in range(4)])


def swap(value, k):
    return lax.ppermute(value, "x", [(i, i ^ k) for i in range(4)])


def shift_upper(value, by):
    return lax.ppermute(value, ("zh", "y"), [(4 + i, 4 + (i + by) % 4) for i in range(4)])


def near(value):
    return pltpu.with_memory_space_constraint(value, pltpu.VMEM)


def local(q_frames, k_frames, v_frames, video_frames, frame_section, frame_offset):
    order = [pltpu.SMEM((16,), jnp.int32), pltpu.SMEM((8,), jnp.int32)]
    kv_send = pl.pallas_call(
        prep_kv_kernel,
        out_shape=jax.ShapeDtypeStruct((64, 32, LANES), jnp.bfloat16),
        in_specs=[smem(), vmem(), vmem()],
        out_specs=vmem(),
        scratch_shapes=order,
        compiler_params=params(VMEM_ALL),
        name="prep_kv",
    )(frame_section, k_frames, v_frames)
    q_send = pl.pallas_call(
        prep_q_kernel,
        out_shape=jax.ShapeDtypeStruct((32, GROUP * 16 + 8, LANES), jnp.bfloat16),
        in_specs=[smem(), smem(), vmem()],
        out_specs=vmem(),
        scratch_shapes=order,
        compiler_params=params(VMEM_ALL),
        name="prep_q",
    )(frame_section, frame_offset, q_frames)
    own = exchange(kv_send, ("zh", "x", "zl", "core"))
    q_send, own = lax.optimization_barrier((q_send, own))
    q_got = exchange(q_send, ("x", "zl", "core"))
    prev, nxt = shift(own, "y", 1), shift(own, "y", -1)
    pieces = [own, prev, nxt, shift(prev[:, :16], "y", 1), shift(nxt[:, 16:], "y", -1)]
    tiles = pl.pallas_call(
        arrange_kernel,
        out_shape=jax.ShapeDtypeStruct((8, 4, 8, 32, LANES), jnp.bfloat16),
        in_specs=[vmem()] * 5,
        out_specs=vmem(),
        compiler_params=params(),
        name="arrange",
    )(*[near(p) for p in pieces])
    tiles, q_got = near(tiles), near(q_got)

    def attend(shifts):
        rows = GROUP * BLOCK
        wide = pltpu.VMEM((TILE, rows), jnp.float32)
        top = pltpu.VMEM((8, rows), jnp.float32)
        line = pltpu.VMEM((1, rows), jnp.float32)
        return pl.pallas_call(
            functools.partial(attend_kernel, shifts),
            out_shape=[jax.ShapeDtypeStruct((1, BLOCK, rows), jnp.bfloat16)] * len(shifts),
            in_specs=[smem(), vmem(), vmem()],
            out_specs=[vmem()] * len(shifts),
            scratch_shapes=[
                pltpu.VMEM((LANES, rows), jnp.bfloat16),
                pltpu.VMEM((TILE, LANES), jnp.float32),
                wide,
                wide,
                top,
                top,
                line,
                line,
                pltpu.VMEM((LANES, rows), jnp.float32),
            ],
            compiler_params=params(),
            cost_estimate=pl.CostEstimate(
                flops=2 * 2 * rows * 4096 * LANES,
                transcendentals=rows * 4096,
                bytes_accessed=3 << 20,
            ),
            name="attend",
        )(video_frames, q_got, tiles)

    parts = {}
    for pair in ((1, 2), (3,), (0,)):
        blocks = attend(pair)
        for part, k in zip(blocks, pair):
            parts[k] = swap(part, k) if k else part
    return pl.pallas_call(
        join_kernel,
        out_shape=jax.ShapeDtypeStruct((1, BLOCK, HEADS_KV * GROUP * LANES), jnp.bfloat16),
        in_specs=[vmem()] * 4,
        out_specs=vmem(),
        compiler_params=params(),
        name="join",
    )(*[near(parts[k]) for k in range(4)])


def solution(mesh):
    fine = Mesh(mesh.devices.reshape(4, 2, 2, 4, 4), ("zl", "core", "zh", "x", "y"))
    ctx = ("zh", "x", "y")
    return jax.shard_map(
        local,
        mesh=fine,
        in_specs=(
            P(SEC, ctx, None, None),
            P(SEC, ctx, None, None),
            P(SEC, ctx, None, None),
            P(),
            P(SEC, ctx),
            P(SEC, ctx),
        ),
        out_specs=P(SEC, ctx, None),
        check_vma=False,
    )
```

```python
import functools
import math

import jax
import jax.numpy as jnp
from jax import lax
from jax.experimental import pallas as pl
from jax.experimental.pallas import tpu as pltpu
from jax.sharding import Mesh, PartitionSpec as P

SEC = ("zl", "core")
BLOCK = 128
LANES = 128
GROUP = 7
HEADS_KV = 4
NEG = -1e30
VMEM_LIMIT = 24 * 1024 * 1024
VMEM_ALL = 56 * 1024 * 1024
TILE = 512


def slot_order(sec_ref, order_ref, count_ref):
    for s in range(8):
        count_ref[s] = 0

    def body(i, _):
        s = sec_ref[0, i]
        c = count_ref[s]
        order_ref[2 * s + c] = i
        count_ref[s] = c + 1
        return 0

    lax.fori_loop(0, 16, body, 0)


def prep_kv_kernel(sec_ref, k_ref, v_ref, out_ref, order_ref, count_ref):
    slot_order(sec_ref, order_ref, count_ref)
    for s in range(8):
        a, b = order_ref[2 * s], order_ref[2 * s + 1]
        for row, ref in ((0, k_ref), (16, v_ref)):
            both = jnp.concatenate([ref[0, a], ref[0, b]], axis=0)
            for h in range(HEADS_KV):
                for zh in range(2):
                    out_ref[(zh * 4 + h) * 8 + s, row : row + 16, :] = both[:, h * LANES : (h + 1) * LANES]


def prep_q_kernel(sec_ref, off_ref, q_ref, out_ref, order_ref, count_ref):
    slot_order(sec_ref, order_ref, count_ref)
    me = lax.axis_index("zl") * 2 + lax.axis_index("core")
    rel = lax.broadcasted_iota(jnp.int32, (8, LANES), 1) - 16 * me
    for s in range(8):
        a, b = order_ref[2 * s], order_ref[2 * s + 1]
        pos_a = jnp.bitwise_and(off_ref[0, a], BLOCK - 1)
        pos_b = jnp.bitwise_and(off_ref[0, b], BLOCK - 1)
        pos = jnp.where(rel < 8, pos_a + rel, pos_b + rel - 8)
        pos = jnp.where((rel >= 0) & (rel < 16), pos, 0)
        pos = pos.astype(jnp.float32).astype(jnp.bfloat16)
        both = jnp.concatenate([q_ref[0, a], q_ref[0, b]], axis=0)
        for h in range(HEADS_KV):
            for g in range(GROUP):
                col = (h * GROUP + g) * LANES
                out_ref[h * 8 + s, g * 16 : (g + 1) * 16, :] = both[:, col : col + LANES]
            out_ref[h * 8 + s, GROUP * 16 :, :] = pos


def arrange_kernel(*refs):
    sources, kv_ref = refs[:5], refs[5]
    copies = []
    for p in range(2):
        own, prev, nxt, far_k, far_v = sources
        for xp in range(4):
            at = pl.ds((p * 4 + xp) * 8, 8)
            for a, src in enumerate((own, prev, nxt)):
                copies.append((src.at[at], kv_ref.at[p * 4 + xp, a]))
            copies.append((far_k.at[at], kv_ref.at[p * 4 + xp, 3, :, 0:16]))
            copies.append((far_v.at[at], kv_ref.at[p * 4 + xp, 3, :, 16:32]))
    for src, dst in copies:
        dst[...] = src[...]


def attend_kernel(
    shifts, video_ref, q_ref, kv_ref, *refs
):
    out_refs = refs[: len(shifts)]
    q_s, mask_s, s0, s1, top0, top1, max_s, sum_s, acc_s = refs[len(shifts) :]
    x, y, zh = lax.axis_index("x"), lax.axis_index("y"), lax.axis_index("zh")
    me = lax.axis_index("zl") * 2 + lax.axis_index("core")
    live = video_ref[me] * 8
    rows = GROUP * BLOCK
    factor = math.log2(math.e) / math.sqrt(128.0)
    down = lax.broadcasted_iota(jnp.int32, (BLOCK, LANES), 0)

    def dot(a, b, ca, cb):
        return lax.dot_general(
            a, b, (((ca,), (cb,)), ((), ())), preferred_element_type=jnp.float32
        )

    def scores(t, s_ref, top_ref):
        s = dot(kv_ref[t, :, :, 0:16, :].reshape(TILE, LANES), q_s[...], 1, 0)
        s_ref[...] = s
        top_ref[...] = jnp.max(s.reshape(TILE // 8, 8, rows), axis=0)

    def absorb(t, s, top):
        old = max_s[...]
        new = jnp.maximum(old, jnp.max(top, axis=0, keepdims=True) * factor)
        keep = jnp.exp2(old - new)
        max_s[...] = new
        p = jnp.exp2(s * factor - new)
        sum_s[...] = sum_s[...] * keep + jnp.sum(p, axis=0, keepdims=True)
        mixed = dot(kv_ref[t, :, :, 16:32, :].reshape(TILE, LANES), p.astype(jnp.bfloat16), 0, 0)
        acc_s[...] = acc_s[...] * keep + mixed

    def absorb_last(t, s_ref):
        s = s_ref[...] + jnp.concatenate([mask_s[...]] * GROUP, axis=1)
        absorb(t, s, jnp.max(s.reshape(TILE // 8, 8, rows), axis=0))

    def one_block(out_ref, xb):
        block = zh * 16 + xb * 4 + y
        block_live = block * BLOCK < live

        @pl.when(jnp.logical_not(block_live))
        def _():
            out_ref[0] = jnp.zeros((BLOCK, rows), jnp.bfloat16)

        @pl.when(block_live)
        def _():
            first = 0
            last = zh * 4 + xb
            meta = q_ref[pl.ds(xb * 8, 8), GROUP * 16 :, :].astype(jnp.float32)
            pos = jnp.sum(meta, axis=0)[0:1]
            for g in range(GROUP):
                raw = q_ref[pl.ds(xb * 8, 8), g * 16 : (g + 1) * 16, :]
                q_s[:, g * BLOCK : (g + 1) * BLOCK] = raw.reshape(BLOCK, LANES).T
            query_pos = jnp.broadcast_to(pos, (BLOCK, LANES))
            key_pos = query_pos.T
            live_rows = (live - block * BLOCK).astype(jnp.float32)
            reach = (key_pos <= query_pos) & (key_pos < live_rows)
            mask_s[0:BLOCK, :] = jnp.where(reach, 0.0, NEG)
            for a, by in ((1, 3), (2, 1), (3, 2)):
                before = jnp.bitwise_and(y + by, 3) < y
                mask_s[a * BLOCK : (a + 1) * BLOCK, :] = jnp.full(
                    (BLOCK, LANES), jnp.where(before, 0.0, NEG)
                )
            max_s[...] = jnp.full((1, rows), NEG, jnp.float32)
            sum_s[...] = jnp.zeros((1, rows), jnp.float32)
            acc_s[...] = jnp.zeros((LANES, rows), jnp.float32)

            if len(shifts) > 1:
                bufs = ((s0, top0), (s1, top1))
                scores(first, s0, top0)

                @pl.when(zh == 1)
                def _():
                    for t in range(4):
                        scores(t + 1, *bufs[(t + 1) % 2])
                        absorb(t, bufs[t % 2][0][...], bufs[t % 2][1][...])

                own = zh * 4
                for n in range(4):

                    @pl.when(xb == n)
                    def _():
                        for t in range(n):
                            scores(own + t + 1, *bufs[(t + 1) % 2])
                            absorb(own + t, bufs[t % 2][0][...], bufs[t % 2][1][...])
                        absorb_last(last, bufs[n % 2][0])

            else:
                scores(first, s0, top0)
                full = last - first

                def pair(n, _):
                    t = first + 2 * n
                    scores(t + 1, s1, top1)
                    absorb(t, s0[...], top0[...])
                    scores(t + 2, s0, top0)
                    absorb(t + 1, s1[...], top1[...])
                    return 0

                lax.fori_loop(0, lax.shift_right_logical(full, 1), pair, 0)
                odd = jnp.bitwise_and(full, 1) == 1

                @pl.when(odd)
                def _():
                    scores(last, s1, top1)
                    absorb(last - 1, s0[...], top0[...])
                    absorb_last(last, s1)

                @pl.when(jnp.logical_not(odd))
                def _():
                    absorb_last(last, s0)

            pick = (down.astype(jnp.float32) == pos).astype(jnp.float32).astype(jnp.bfloat16)
            scale = 1.0 / sum_s[...]
            for g in range(GROUP):
                at = slice(g * BLOCK, (g + 1) * BLOCK)
                piece = jnp.where(pos < live_rows, acc_s[:, at] * scale[:, at], 0.0)
                out_ref[0, :, g * LANES : (g + 1) * LANES] = dot(
                    pick, piece.astype(jnp.bfloat16), 1, 1
                ).astype(jnp.bfloat16)

    for out_ref, k in zip(out_refs, shifts):
        one_block(out_ref, jnp.bitwise_xor(x, k))


def attend_scratch():
    rows = GROUP * BLOCK
    wide = pltpu.VMEM((TILE, rows), jnp.float32)
    top = pltpu.VMEM((8, rows), jnp.float32)
    line = pltpu.VMEM((1, rows), jnp.float32)
    queries = pltpu.VMEM((LANES, rows), jnp.bfloat16)
    mask = pltpu.VMEM((TILE, LANES), jnp.float32)
    total = pltpu.VMEM((LANES, rows), jnp.float32)
    return [queries, mask, wide, wide, top, top, line, line, total]


def join_kernel(a_ref, b_ref, c_ref, d_ref, out_ref):
    x = lax.axis_index("x")
    for k, ref in enumerate((a_ref, b_ref, c_ref, d_ref)):
        head = jnp.bitwise_xor(x, k)
        col = pl.multiple_of(head * (GROUP * LANES), LANES)
        out_ref[0, :, pl.ds(col, GROUP * LANES)] = ref[0]


def vmem():
    return pl.BlockSpec(memory_space=pltpu.VMEM)


def smem():
    return pl.BlockSpec(memory_space=pltpu.SMEM)


def anywhere():
    return pl.BlockSpec(memory_space=pl.ANY)


def params(limit=VMEM_LIMIT):
    return pltpu.CompilerParams(vmem_limit_bytes=limit)


def exchange(value, axes):
    return lax.all_to_all(value, axes, split_axis=0, concat_axis=0, tiled=True)


def shift(value, axis, by):
    return lax.ppermute(value, axis, [(i, (i + by) % 4) for i in range(4)])


def swap(value, k):
    return lax.ppermute(value, "x", [(i, i ^ k) for i in range(4)])


def shift_upper(value, by):
    return lax.ppermute(value, ("zh", "y"), [(4 + i, 4 + (i + by) % 4) for i in range(4)])


def near(value):
    return pltpu.with_memory_space_constraint(value, pltpu.VMEM)


def local(q_frames, k_frames, v_frames, video_frames, frame_section, frame_offset):
    order = [pltpu.SMEM((16,), jnp.int32), pltpu.SMEM((8,), jnp.int32)]
    kv_send = pl.pallas_call(
        prep_kv_kernel,
        out_shape=jax.ShapeDtypeStruct((64, 32, LANES), jnp.bfloat16),
        in_specs=[smem(), vmem(), vmem()],
        out_specs=vmem(),
        scratch_shapes=order,
        compiler_params=params(VMEM_ALL),
        name="prep_kv",
    )(frame_section, k_frames, v_frames)
    q_send = pl.pallas_call(
        prep_q_kernel,
        out_shape=jax.ShapeDtypeStruct((32, GROUP * 16 + 8, LANES), jnp.bfloat16),
        in_specs=[smem(), smem(), vmem()],
        out_specs=vmem(),
        scratch_shapes=order,
        compiler_params=params(VMEM_ALL),
        name="prep_q",
    )(frame_section, frame_offset, q_frames)
    own = exchange(kv_send, ("zh", "x", "zl", "core"))
    q_send, own = lax.optimization_barrier((q_send, own))
    q_got = exchange(q_send, ("x", "zl", "core"))
    prev, nxt = shift(own, "y", 1), shift(own, "y", -1)
    pieces = [own, prev, nxt, shift(prev[:, :16], "y", 1), shift(nxt[:, 16:], "y", -1)]
    tiles = pl.pallas_call(
        arrange_kernel,
        out_shape=jax.ShapeDtypeStruct((8, 4, 8, 32, LANES), jnp.bfloat16),
        in_specs=[vmem()] * 5,
        out_specs=vmem(),
        compiler_params=params(),
        name="arrange",
    )(*[near(p) for p in pieces])
    tiles, q_got = near(tiles), near(q_got)

    def attend(shifts):
        rows = GROUP * BLOCK
        return pl.pallas_call(
            functools.partial(attend_kernel, shifts),
            out_shape=[jax.ShapeDtypeStruct((1, BLOCK, rows), jnp.bfloat16)] * len(shifts),
            in_specs=[smem(), vmem(), vmem()],
            out_specs=[vmem()] * len(shifts),
            scratch_shapes=attend_scratch(),
            compiler_params=params(),
            cost_estimate=pl.CostEstimate(
                flops=2 * 2 * rows * 4096 * LANES,
                transcendentals=rows * 4096,
                bytes_accessed=3 << 20,
            ),
            name="attend",
        )(video_frames, q_got, tiles)

    parts = {}
    for pair in ((1, 2), (3,), (0,)):
        blocks = attend(pair)
        for part, k in zip(blocks, pair):
            parts[k] = swap(part, k) if k else part
    return pl.pallas_call(
        join_kernel,
        out_shape=jax.ShapeDtypeStruct((1, BLOCK, HEADS_KV * GROUP * LANES), jnp.bfloat16),
        in_specs=[vmem()] * 4,
        out_specs=vmem(),
        compiler_params=params(),
        name="join",
    )(*[near(parts[k]) for k in range(4)])


def solution(mesh):
    fine = Mesh(mesh.devices.reshape(4, 2, 2, 4, 4), ("zl", "core", "zh", "x", "y"))
    ctx = ("zh", "x", "y")
    return jax.shard_map(
        local,
        mesh=fine,
        in_specs=(
            P(SEC, ctx, None, None),
            P(SEC, ctx, None, None),
            P(SEC, ctx, None, None),
            P(),
            P(SEC, ctx),
            P(SEC, ctx),
        ),
        out_specs=P(SEC, ctx, None),
        check_vma=False,
    )
```

```python
import functools
import math

import jax
import jax.numpy as jnp
from jax import lax
from jax.experimental import pallas as pl
from jax.experimental.pallas import tpu as pltpu
from jax.sharding import Mesh, PartitionSpec as P

SEC = ("zl", "core")
BLOCK = 128
LANES = 128
GROUP = 7
HEADS_KV = 4
NEG = -1e30
VMEM_LIMIT = 24 * 1024 * 1024
VMEM_ALL = 56 * 1024 * 1024
TILE = 512


def slot_order(sec_ref, order_ref, count_ref):
    for s in range(8):
        count_ref[s] = 0

    def body(i, _):
        s = sec_ref[0, i]
        c = count_ref[s]
        order_ref[2 * s + c] = i
        count_ref[s] = c + 1
        return 0

    lax.fori_loop(0, 16, body, 0)


def prep_kv_kernel(sec_ref, k_ref, v_ref, out_ref, order_ref, count_ref):
    slot_order(sec_ref, order_ref, count_ref)
    for s in range(8):
        a, b = order_ref[2 * s], order_ref[2 * s + 1]
        for row, ref in ((0, k_ref), (16, v_ref)):
            both = jnp.concatenate([ref[0, a], ref[0, b]], axis=0)
            for h in range(HEADS_KV):
                for zh in range(2):
                    out_ref[(zh * 4 + h) * 8 + s, row : row + 16, :] = both[:, h * LANES : (h + 1) * LANES]


def prep_q_kernel(sec_ref, off_ref, q_ref, out_ref, order_ref, count_ref):
    slot_order(sec_ref, order_ref, count_ref)
    me = lax.axis_index("zl") * 2 + lax.axis_index("core")
    rel = lax.broadcasted_iota(jnp.int32, (8, LANES), 1) - 16 * me
    for s in range(8):
        a, b = order_ref[2 * s], order_ref[2 * s + 1]
        pos_a = jnp.bitwise_and(off_ref[0, a], BLOCK - 1)
        pos_b = jnp.bitwise_and(off_ref[0, b], BLOCK - 1)
        pos = jnp.where(rel < 8, pos_a + rel, pos_b + rel - 8)
        pos = jnp.where((rel >= 0) & (rel < 16), pos, 0)
        pos = pos.astype(jnp.float32).astype(jnp.bfloat16)
        both = jnp.concatenate([q_ref[0, a], q_ref[0, b]], axis=0)
        for h in range(HEADS_KV):
            for g in range(GROUP):
                col = (h * GROUP + g) * LANES
                out_ref[h * 8 + s, g * 16 : (g + 1) * 16, :] = both[:, col : col + LANES]
            out_ref[h * 8 + s, GROUP * 16 :, :] = pos


def arrange_kernel(*refs):
    sources, kv_ref = refs[:5], refs[5]
    copies = []
    for p in range(2):
        own, prev, nxt, far_k, far_v = sources
        for xp in range(4):
            at = pl.ds((p * 4 + xp) * 8, 8)
            for a, src in enumerate((own, prev, nxt)):
                copies.append((src.at[at], kv_ref.at[p * 4 + xp, a]))
            copies.append((far_k.at[at], kv_ref.at[p * 4 + xp, 3, :, 0:16]))
            copies.append((far_v.at[at], kv_ref.at[p * 4 + xp, 3, :, 16:32]))
    for src, dst in copies:
        dst[...] = src[...]


def attend_kernel(
    shifts, video_ref, q_ref, kv_ref, *refs
):
    out_refs = refs[: len(shifts)]
    q_s, mask_s, s0, s1, top0, top1, max_s, acc_s = refs[len(shifts) :]
    x, y, zh = lax.axis_index("x"), lax.axis_index("y"), lax.axis_index("zh")
    me = lax.axis_index("zl") * 2 + lax.axis_index("core")
    live = video_ref[me] * 8
    rows = GROUP * BLOCK
    factor = math.log2(math.e) / math.sqrt(128.0)
    down = lax.broadcasted_iota(jnp.int32, (BLOCK, LANES), 0)

    def dot(a, b, ca, cb):
        return lax.dot_general(
            a, b, (((ca,), (cb,)), ((), ())), preferred_element_type=jnp.float32
        )

    def scores(t, s_ref, top_ref):
        s = dot(kv_ref[t, :, :, 0:16, :].reshape(TILE, LANES), q_s[...], 1, 0)
        s_ref[...] = s
        top_ref[...] = jnp.max(s.reshape(TILE // 8, 8, rows), axis=0)

    def absorb(t, s, top):
        old = max_s[...]
        new = jnp.maximum(old, jnp.max(top, axis=0, keepdims=True) * factor)
        keep = jnp.exp2(old - new)
        max_s[...] = new
        p = jnp.exp2(s * factor - new)
        values = kv_ref[t, :, :, 16:32, :].reshape(TILE, LANES)
        ones = jnp.ones((8, TILE), jnp.bfloat16)
        values = jnp.concatenate([values.T, ones], axis=0)
        acc_s[...] = acc_s[...] * keep + dot(values, p.astype(jnp.bfloat16), 1, 0)

    def absorb_last(t, s_ref):
        s = s_ref[...] + jnp.concatenate([mask_s[...]] * GROUP, axis=1)
        absorb(t, s, jnp.max(s.reshape(TILE // 8, 8, rows), axis=0))

    def one_block(out_ref, xb):
        block = zh * 16 + xb * 4 + y
        block_live = block * BLOCK < live

        @pl.when(jnp.logical_not(block_live))
        def _():
            out_ref[0] = jnp.zeros((BLOCK, rows), jnp.bfloat16)

        @pl.when(block_live)
        def _():
            first = 0
            last = zh * 4 + xb
            meta = q_ref[pl.ds(xb * 8, 8), GROUP * 16 :, :].astype(jnp.float32)
            pos = jnp.sum(meta, axis=0)[0:1]
            for g in range(GROUP):
                raw = q_ref[pl.ds(xb * 8, 8), g * 16 : (g + 1) * 16, :]
                q_s[:, g * BLOCK : (g + 1) * BLOCK] = raw.reshape(BLOCK, LANES).T
            query_pos = jnp.broadcast_to(pos, (BLOCK, LANES))
            key_pos = query_pos.T
            live_rows = (live - block * BLOCK).astype(jnp.float32)
            reach = (key_pos <= query_pos) & (key_pos < live_rows)
            mask_s[0:BLOCK, :] = jnp.where(reach, 0.0, NEG)
            for a, by in ((1, 3), (2, 1), (3, 2)):
                before = jnp.bitwise_and(y + by, 3) < y
                mask_s[a * BLOCK : (a + 1) * BLOCK, :] = jnp.full(
                    (BLOCK, LANES), jnp.where(before, 0.0, NEG)
                )
            max_s[...] = jnp.full((1, rows), NEG, jnp.float32)
            acc_s[...] = jnp.zeros((LANES + 8, rows), jnp.float32)

            scores(first, s0, top0)
            full = last - first

            def pair(n, _):
                t = first + 2 * n
                scores(t + 1, s1, top1)
                absorb(t, s0[...], top0[...])
                scores(t + 2, s0, top0)
                absorb(t + 1, s1[...], top1[...])
                return 0

            lax.fori_loop(0, lax.shift_right_logical(full, 1), pair, 0)
            odd = jnp.bitwise_and(full, 1) == 1

            @pl.when(odd)
            def _():
                scores(last, s1, top1)
                absorb(last - 1, s0[...], top0[...])
                absorb_last(last, s1)

            @pl.when(jnp.logical_not(odd))
            def _():
                absorb_last(last, s0)

            pick = (down.astype(jnp.float32) == pos).astype(jnp.float32).astype(jnp.bfloat16)
            scale = 1.0 / acc_s[LANES : LANES + 1, :]
            for g in range(GROUP):
                at = slice(g * BLOCK, (g + 1) * BLOCK)
                piece = jnp.where(pos < live_rows, acc_s[0:LANES, at] * scale[:, at], 0.0)
                out_ref[0, :, g * LANES : (g + 1) * LANES] = dot(
                    pick, piece.astype(jnp.bfloat16), 1, 1
                ).astype(jnp.bfloat16)

    for out_ref, k in zip(out_refs, shifts):
        one_block(out_ref, jnp.bitwise_xor(x, k))


def attend_scratch():
    rows = GROUP * BLOCK
    wide = pltpu.VMEM((TILE, rows), jnp.float32)
    top = pltpu.VMEM((8, rows), jnp.float32)
    line = pltpu.VMEM((1, rows), jnp.float32)
    queries = pltpu.VMEM((LANES, rows), jnp.bfloat16)
    mask = pltpu.VMEM((TILE, LANES), jnp.float32)
    total = pltpu.VMEM((LANES + 8, rows), jnp.float32)
    return [queries, mask, wide, wide, top, top, line, total]


def join_kernel(a_ref, b_ref, c_ref, d_ref, out_ref):
    x = lax.axis_index("x")
    for k, ref in enumerate((a_ref, b_ref, c_ref, d_ref)):
        head = jnp.bitwise_xor(x, k)
        col = pl.multiple_of(head * (GROUP * LANES), LANES)
        out_ref[0, :, pl.ds(col, GROUP * LANES)] = ref[0]


def vmem():
    return pl.BlockSpec(memory_space=pltpu.VMEM)


def smem():
    return pl.BlockSpec(memory_space=pltpu.SMEM)


def anywhere():
    return pl.BlockSpec(memory_space=pl.ANY)


def params(limit=VMEM_LIMIT):
    return pltpu.CompilerParams(vmem_limit_bytes=limit)


def exchange(value, axes):
    return lax.all_to_all(value, axes, split_axis=0, concat_axis=0, tiled=True)


def shift(value, axis, by):
    return lax.ppermute(value, axis, [(i, (i + by) % 4) for i in range(4)])


def swap(value, k):
    return lax.ppermute(value, "x", [(i, i ^ k) for i in range(4)])


def shift_upper(value, by):
    return lax.ppermute(value, ("zh", "y"), [(4 + i, 4 + (i + by) % 4) for i in range(4)])


def near(value):
    return pltpu.with_memory_space_constraint(value, pltpu.VMEM)


def local(q_frames, k_frames, v_frames, video_frames, frame_section, frame_offset):
    order = [pltpu.SMEM((16,), jnp.int32), pltpu.SMEM((8,), jnp.int32)]
    kv_send = pl.pallas_call(
        prep_kv_kernel,
        out_shape=jax.ShapeDtypeStruct((64, 32, LANES), jnp.bfloat16),
        in_specs=[smem(), vmem(), vmem()],
        out_specs=vmem(),
        scratch_shapes=order,
        compiler_params=params(VMEM_ALL),
        name="prep_kv",
    )(frame_section, k_frames, v_frames)
    q_send = pl.pallas_call(
        prep_q_kernel,
        out_shape=jax.ShapeDtypeStruct((32, GROUP * 16 + 8, LANES), jnp.bfloat16),
        in_specs=[smem(), smem(), vmem()],
        out_specs=vmem(),
        scratch_shapes=order,
        compiler_params=params(VMEM_ALL),
        name="prep_q",
    )(frame_section, frame_offset, q_frames)
    own = exchange(kv_send, ("zh", "x", "zl", "core"))
    q_send, own = lax.optimization_barrier((q_send, own))
    q_got = exchange(q_send, ("x", "zl", "core"))
    prev, nxt = shift(own, "y", 1), shift(own, "y", -1)
    pieces = [own, prev, nxt, shift(prev[:, :16], "y", 1), shift(nxt[:, 16:], "y", -1)]
    tiles = pl.pallas_call(
        arrange_kernel,
        out_shape=jax.ShapeDtypeStruct((8, 4, 8, 32, LANES), jnp.bfloat16),
        in_specs=[vmem()] * 5,
        out_specs=vmem(),
        compiler_params=params(),
        name="arrange",
    )(*[near(p) for p in pieces])
    tiles, q_got = near(tiles), near(q_got)

    def attend(shifts):
        rows = GROUP * BLOCK
        return pl.pallas_call(
            functools.partial(attend_kernel, shifts),
            out_shape=[jax.ShapeDtypeStruct((1, BLOCK, rows), jnp.bfloat16)] * len(shifts),
            in_specs=[smem(), vmem(), vmem()],
            out_specs=[vmem()] * len(shifts),
            scratch_shapes=attend_scratch(),
            compiler_params=params(),
            cost_estimate=pl.CostEstimate(
                flops=2 * 2 * rows * 4096 * LANES,
                transcendentals=rows * 4096,
                bytes_accessed=3 << 20,
            ),
            name="attend",
        )(video_frames, q_got, tiles)

    parts = {}
    for pair in ((2,), (1, 3), (0,)):
        blocks = attend(pair)
        for part, k in zip(blocks, pair):
            parts[k] = swap(part, k) if k else part
    return pl.pallas_call(
        join_kernel,
        out_shape=jax.ShapeDtypeStruct((1, BLOCK, HEADS_KV * GROUP * LANES), jnp.bfloat16),
        in_specs=[vmem()] * 4,
        out_specs=vmem(),
        compiler_params=params(),
        name="join",
    )(*[near(parts[k]) for k in range(4)])


def solution(mesh):
    fine = Mesh(mesh.devices.reshape(4, 2, 2, 4, 4), ("zl", "core", "zh", "x", "y"))
    ctx = ("zh", "x", "y")
    return jax.shard_map(
        local,
        mesh=fine,
        in_specs=(
            P(SEC, ctx, None, None),
            P(SEC, ctx, None, None),
            P(SEC, ctx, None, None),
            P(),
            P(SEC, ctx),
            P(SEC, ctx),
        ),
        out_specs=P(SEC, ctx, None),
        check_vma=False,
    )
```

```python
import functools
import math

import jax
import jax.numpy as jnp
from jax import lax
from jax.experimental import pallas as pl
from jax.experimental.pallas import tpu as pltpu
from jax.sharding import Mesh, PartitionSpec as P

SEC = ("zl", "core")
BLOCK = 128
LANES = 128
GROUP = 7
HEADS_KV = 4
NEG = -1e30
VMEM_LIMIT = 24 * 1024 * 1024
VMEM_ALL = 56 * 1024 * 1024
TILE = 512


def slot_order(sec_ref, order_ref, count_ref):
    for s in range(8):
        count_ref[s] = 0

    def body(i, _):
        s = sec_ref[0, i]
        c = count_ref[s]
        order_ref[2 * s + c] = i
        count_ref[s] = c + 1
        return 0

    lax.fori_loop(0, 16, body, 0)


def prep_kv_kernel(sec_ref, k_ref, v_ref, out_ref, order_ref, count_ref):
    slot_order(sec_ref, order_ref, count_ref)
    for s in range(8):
        a, b = order_ref[2 * s], order_ref[2 * s + 1]
        for row, ref in ((0, k_ref), (16, v_ref)):
            both = jnp.concatenate([ref[0, a], ref[0, b]], axis=0)
            for h in range(HEADS_KV):
                for zh in range(2):
                    out_ref[(zh * 4 + h) * 8 + s, row : row + 16, :] = both[:, h * LANES : (h + 1) * LANES]


def prep_q_kernel(sec_ref, off_ref, q_ref, out_ref, order_ref, count_ref):
    slot_order(sec_ref, order_ref, count_ref)
    me = lax.axis_index("zl") * 2 + lax.axis_index("core")
    rel = lax.broadcasted_iota(jnp.int32, (8, LANES), 1) - 16 * me
    for s in range(8):
        a, b = order_ref[2 * s], order_ref[2 * s + 1]
        pos_a = jnp.bitwise_and(off_ref[0, a], BLOCK - 1)
        pos_b = jnp.bitwise_and(off_ref[0, b], BLOCK - 1)
        pos = jnp.where(rel < 8, pos_a + rel, pos_b + rel - 8)
        pos = jnp.where((rel >= 0) & (rel < 16), pos, 0)
        pos = pos.astype(jnp.float32).astype(jnp.bfloat16)
        both = jnp.concatenate([q_ref[0, a], q_ref[0, b]], axis=0)
        for h in range(HEADS_KV):
            for g in range(GROUP):
                col = (h * GROUP + g) * LANES
                out_ref[h * 8 + s, g * 16 : (g + 1) * 16, :] = both[:, col : col + LANES]
            out_ref[h * 8 + s, GROUP * 16 :, :] = pos


def arrange_kernel(*refs):
    sources, kv_ref = refs[:5], refs[5]
    copies = []
    for p in range(2):
        own, prev, nxt, far_k, far_v = sources
        for xp in range(4):
            at = pl.ds((p * 4 + xp) * 8, 8)
            for a, src in enumerate((own, prev, nxt)):
                copies.append((src.at[at], kv_ref.at[p * 4 + xp, a]))
            copies.append((far_k.at[at], kv_ref.at[p * 4 + xp, 3, :, 0:16]))
            copies.append((far_v.at[at], kv_ref.at[p * 4 + xp, 3, :, 16:32]))
    for src, dst in copies:
        dst[...] = src[...]


def attend_kernel(
    shifts, video_ref, q_ref, kv_ref, *refs
):
    out_refs = refs[: len(shifts)]
    got_s, q_s, mask_s, s0, s1, top0, top1, max_s, acc_s, sem = refs[len(shifts) :]
    x, y, zh = lax.axis_index("x"), lax.axis_index("y"), lax.axis_index("zh")
    me = lax.axis_index("zl") * 2 + lax.axis_index("core")
    live = video_ref[me] * 8
    copies = []
    for i, k in enumerate(shifts):
        at = pl.ds(jnp.bitwise_xor(x, k) * 8, 8)
        copies.append(pltpu.make_async_copy(q_ref.at[at], got_s.at[i], sem.at[i]))
        copies[-1].start()
    rows = GROUP * BLOCK
    factor = math.log2(math.e) / math.sqrt(128.0)
    down = lax.broadcasted_iota(jnp.int32, (BLOCK, LANES), 0)

    def dot(a, b, ca, cb):
        return lax.dot_general(
            a, b, (((ca,), (cb,)), ((), ())), preferred_element_type=jnp.float32
        )

    def scores(t, s_ref, top_ref):
        s = dot(kv_ref[t, :, :, 0:16, :].reshape(TILE, LANES), q_s[...], 1, 0)
        s_ref[...] = s
        top_ref[...] = jnp.max(s.reshape(TILE // 8, 8, rows), axis=0)

    def absorb(t, s, top):
        old = max_s[...]
        new = jnp.maximum(old, jnp.max(top, axis=0, keepdims=True) * factor)
        keep = jnp.exp2(old - new)
        max_s[...] = new
        p = jnp.exp2(s * factor - new)
        values = kv_ref[t, :, :, 16:32, :].reshape(TILE, LANES)
        ones = jnp.ones((8, TILE), jnp.bfloat16)
        values = jnp.concatenate([values.T, ones], axis=0)
        acc_s[...] = acc_s[...] * keep + dot(values, p.astype(jnp.bfloat16), 1, 0)

    def absorb_last(t, s_ref):
        s = s_ref[...] + jnp.concatenate([mask_s[...]] * GROUP, axis=1)
        absorb(t, s, jnp.max(s.reshape(TILE // 8, 8, rows), axis=0))

    def one_block(out_ref, got_ref, xb):
        block = zh * 16 + xb * 4 + y
        block_live = block * BLOCK < live

        @pl.when(jnp.logical_not(block_live))
        def _():
            out_ref[0] = jnp.zeros((BLOCK, rows), jnp.bfloat16)

        @pl.when(block_live)
        def _():
            first = 0
            last = zh * 4 + xb
            meta = got_ref[:, GROUP * 16 :, :].astype(jnp.float32)
            pos = jnp.sum(meta, axis=0)[0:1]
            for g in range(GROUP):
                raw = got_ref[:, g * 16 : (g + 1) * 16, :]
                q_s[:, g * BLOCK : (g + 1) * BLOCK] = raw.reshape(BLOCK, LANES).T
            query_pos = jnp.broadcast_to(pos, (BLOCK, LANES))
            key_pos = query_pos.T
            live_rows = (live - block * BLOCK).astype(jnp.float32)
            reach = (key_pos <= query_pos) & (key_pos < live_rows)
            mask_s[0:BLOCK, :] = jnp.where(reach, 0.0, NEG)
            for a, by in ((1, 3), (2, 1), (3, 2)):
                before = jnp.bitwise_and(y + by, 3) < y
                mask_s[a * BLOCK : (a + 1) * BLOCK, :] = jnp.full(
                    (BLOCK, LANES), jnp.where(before, 0.0, NEG)
                )
            max_s[...] = jnp.full((1, rows), NEG, jnp.float32)
            acc_s[...] = jnp.zeros((LANES + 8, rows), jnp.float32)

            scores(first, s0, top0)
            full = last - first

            def pair(n, _):
                t = first + 2 * n
                scores(t + 1, s1, top1)
                absorb(t, s0[...], top0[...])
                scores(t + 2, s0, top0)
                absorb(t + 1, s1[...], top1[...])
                return 0

            lax.fori_loop(0, lax.shift_right_logical(full, 1), pair, 0)
            odd = jnp.bitwise_and(full, 1) == 1

            @pl.when(odd)
            def _():
                scores(last, s1, top1)
                absorb(last - 1, s0[...], top0[...])
                absorb_last(last, s1)

            @pl.when(jnp.logical_not(odd))
            def _():
                absorb_last(last, s0)

            pick = (down.astype(jnp.float32) == pos).astype(jnp.float32).astype(jnp.bfloat16)
            scale = 1.0 / acc_s[LANES : LANES + 1, :]
            for g in range(GROUP):
                at = slice(g * BLOCK, (g + 1) * BLOCK)
                piece = jnp.where(pos < live_rows, acc_s[0:LANES, at] * scale[:, at], 0.0)
                out_ref[0, :, g * LANES : (g + 1) * LANES] = dot(
                    pick, piece.astype(jnp.bfloat16), 1, 1
                ).astype(jnp.bfloat16)

    for i, k in enumerate(shifts):
        copies[i].wait()
        one_block(out_refs[i], got_s.at[i], jnp.bitwise_xor(x, k))


def attend_scratch(blocks):
    rows = GROUP * BLOCK
    wide = pltpu.VMEM((TILE, rows), jnp.float32)
    top = pltpu.VMEM((8, rows), jnp.float32)
    line = pltpu.VMEM((1, rows), jnp.float32)
    queries = pltpu.VMEM((LANES, rows), jnp.bfloat16)
    mask = pltpu.VMEM((TILE, LANES), jnp.float32)
    total = pltpu.VMEM((LANES + 8, rows), jnp.float32)
    got = pltpu.VMEM((blocks, 8, GROUP * 16 + 8, LANES), jnp.bfloat16)
    sem = pltpu.SemaphoreType.DMA((blocks,))
    return [got, queries, mask, wide, wide, top, top, line, total, sem]


def join_kernel(a_ref, b_ref, c_ref, d_ref, out_ref):
    x = lax.axis_index("x")
    for k, ref in enumerate((a_ref, b_ref, c_ref, d_ref)):
        head = jnp.bitwise_xor(x, k)
        col = pl.multiple_of(head * (GROUP * LANES), LANES)
        out_ref[0, :, pl.ds(col, GROUP * LANES)] = ref[0]


def vmem():
    return pl.BlockSpec(memory_space=pltpu.VMEM)


def smem():
    return pl.BlockSpec(memory_space=pltpu.SMEM)


def anywhere():
    return pl.BlockSpec(memory_space=pl.ANY)


def params(limit=VMEM_LIMIT):
    return pltpu.CompilerParams(vmem_limit_bytes=limit)


def exchange(value, axes):
    return lax.all_to_all(value, axes, split_axis=0, concat_axis=0, tiled=True)


def shift(value, axis, by):
    return lax.ppermute(value, axis, [(i, (i + by) % 4) for i in range(4)])


def swap(value, k):
    return lax.ppermute(value, "x", [(i, i ^ k) for i in range(4)])


def shift_upper(value, by):
    return lax.ppermute(value, ("zh", "y"), [(4 + i, 4 + (i + by) % 4) for i in range(4)])


def near(value):
    return pltpu.with_memory_space_constraint(value, pltpu.VMEM)


def local(q_frames, k_frames, v_frames, video_frames, frame_section, frame_offset):
    order = [pltpu.SMEM((16,), jnp.int32), pltpu.SMEM((8,), jnp.int32)]
    kv_send = pl.pallas_call(
        prep_kv_kernel,
        out_shape=jax.ShapeDtypeStruct((64, 32, LANES), jnp.bfloat16),
        in_specs=[smem(), vmem(), vmem()],
        out_specs=vmem(),
        scratch_shapes=order,
        compiler_params=params(VMEM_ALL),
        name="prep_kv",
    )(frame_section, k_frames, v_frames)
    q_send = pl.pallas_call(
        prep_q_kernel,
        out_shape=jax.ShapeDtypeStruct((32, GROUP * 16 + 8, LANES), jnp.bfloat16),
        in_specs=[smem(), smem(), vmem()],
        out_specs=vmem(),
        scratch_shapes=order,
        compiler_params=params(VMEM_ALL),
        name="prep_q",
    )(frame_section, frame_offset, q_frames)
    own = exchange(kv_send, ("zh", "x", "zl", "core"))
    q_send, own = lax.optimization_barrier((q_send, own))
    q_got = exchange(q_send, ("x", "zl", "core"))
    prev, nxt = shift(own, "y", 1), shift(own, "y", -1)
    pieces = [own, prev, nxt, shift(prev[:, :16], "y", 1), shift(nxt[:, 16:], "y", -1)]
    tiles = pl.pallas_call(
        arrange_kernel,
        out_shape=jax.ShapeDtypeStruct((8, 4, 8, 32, LANES), jnp.bfloat16),
        in_specs=[vmem()] * 5,
        out_specs=vmem(),
        compiler_params=params(),
        name="arrange",
    )(*[near(p) for p in pieces])
    tiles, q_got = near(tiles), near(q_got)

    def attend(shifts):
        rows = GROUP * BLOCK
        return pl.pallas_call(
            functools.partial(attend_kernel, shifts),
            out_shape=[jax.ShapeDtypeStruct((1, BLOCK, rows), jnp.bfloat16)] * len(shifts),
            in_specs=[smem(), anywhere(), vmem()],
            out_specs=[vmem()] * len(shifts),
            scratch_shapes=attend_scratch(len(shifts)),
            compiler_params=params(),
            cost_estimate=pl.CostEstimate(
                flops=2 * 2 * rows * 4096 * LANES,
                transcendentals=rows * 4096,
                bytes_accessed=3 << 20,
            ),
            name="attend",
        )(video_frames, q_got, tiles)

    parts = {}
    for pair in ((2,), (1, 3), (0,)):
        blocks = attend(pair)
        for part, k in zip(blocks, pair):
            parts[k] = swap(part, k) if k else part
    return pl.pallas_call(
        join_kernel,
        out_shape=jax.ShapeDtypeStruct((1, BLOCK, HEADS_KV * GROUP * LANES), jnp.bfloat16),
        in_specs=[vmem()] * 4,
        out_specs=vmem(),
        compiler_params=params(),
        name="join",
    )(*[near(parts[k]) for k in range(4)])


def solution(mesh):
    fine = Mesh(mesh.devices.reshape(4, 2, 2, 4, 4), ("zl", "core", "zh", "x", "y"))
    ctx = ("zh", "x", "y")
    return jax.shard_map(
        local,
        mesh=fine,
        in_specs=(
            P(SEC, ctx, None, None),
            P(SEC, ctx, None, None),
            P(SEC, ctx, None, None),
            P(),
            P(SEC, ctx),
            P(SEC, ctx),
        ),
        out_specs=P(SEC, ctx, None),
        check_vma=False,
    )
```
